32 devices in a mesh: sim: 16 (over z, y, x), learn: 2 (over core).
Axes of the slice: x: 2, y: 2, z: 4, core: 2. Of those that a mesh axis runs over, the one named last changes fastest.
Arguments:
- state_field: float32 [128, 256, 1024], P(None, 'sim', 'learn'), may hold values from -6 to 6
- diffusion: float32 [128], replicated, may hold values from 0.03 to 0.24
- weight_in: float32 [128, 1024], replicated, may hold values from -0.5 to 0.5
- weight_mid: float32 [1024, 1024], replicated, may hold values from -0.1875 to 0.1875
- weight_out: float32 [1024, 128], replicated, may hold values from -0.1875 to 0.1875
- block_tile: int32 [384, 1], P('learn'), may hold values from 0 to 15; in each aligned block of 12 rows (0 to 11, 12 to 23, ...) no two rows name the same one
- block_pos: int32 [384], P('learn'), may hold values from 0 to 63
Outputs:
- new_state: float32 [128, 256, 1024], P(None, 'sim', 'learn')
- new_in: float32 [128, 1024], replicated
- new_mid: float32 [1024, 1024], replicated
- new_out: float32 [1024, 128], replicated
The draws below stay inside these ranges and needn't reach their ends.
Inputs may be any that keep to these rules, and one draw needn't show every extreme that they name: `block_tile`: in each aligned block of 12 rows no tile index appears twice.
All inputs are finite; a program needn't handle non-finite values.
Results may differ from the reference program's by a relative error of at most 0.0003.
The reference program's roundings to bfloat16 on the way (of `inputs`, `targets` and `error`) count: a program that leaves them out, or rounds other values in their place, can miss the bound.
Values may be sent and summed in bfloat16 or wider, within the bound.
A program may use at most 128 MiB of HBM per device.

```python
import math
import jax
import jax.numpy as jnp
import numpy as np
from jax import lax

LEV = 128
HID = 1024
BW = 128
RY = 16
RX = 512
SAMPLES = 12
NY = 256
NX = 1024
REQ = 384
N_SIM = 16


def place_ends(result, stream_key, least, largest):
    extent = result.shape
    place = [jax.random.randint(jax.random.fold_in(stream_key, axis), (), 0, extent[axis]) for axis in range(len(extent))]
    result = result.at[tuple(place)].set(least)
    longest = extent.index(max(extent))
    place[longest] = (place[longest] + 1) % extent[longest]
    return result.at[tuple(place)].set(largest)


def levels(stream_key, shape, cuts, low, top_value):
    level = 1.0
    for axis_at, parts in cuts:
        heights = jax.random.uniform(jax.random.fold_in(jax.random.fold_in(stream_key, 6), axis_at), (parts,), jnp.float32, low / len(cuts), top_value / len(cuts))
        level = level * jnp.repeat(jnp.exp(heights), shape[axis_at] // parts).reshape((-1,) + (1,) * (len(shape) - 1 - axis_at))
    return level


def deal_out(rng, own, number, rows, number_of, top, bound, slope):
    sequence = jax.random.permutation(rng, number_of)
    crowded, ordinary = load_shares(number_of, rows * top, bound, slope, True), load_shares(number_of, rows * top, bound, slope, False)
    places = jnp.arange(number_of)

    def named(sizes, rotation):
        used = int((sizes > 0).sum())
        fixed = max(1, used // 4)
        passed = fixed + (places - fixed + rotation * (used - fixed)) % max(1, number_of - fixed)
        return jnp.zeros((number_of,), jnp.int32).at[sequence[jnp.where(places < fixed, places, passed)]].set(jnp.asarray(sizes, jnp.int32))

    sizes = jnp.where(number % 4 == 0, named(crowded, number // 4), named(ordinary, number - number // 4 - 1))
    mixed = jax.random.permutation(jax.random.fold_in(own, 3), number_of)
    source_of, receiver = mixed[0:number_of // 2 * 2:2], mixed[1:number_of // 2 * 2:2]
    room = jnp.minimum(sizes[source_of] - 1, bound - sizes[receiver]) // 2
    room = jnp.where((source_of == sequence[0]) | (receiver == sequence[0]) | (sizes[receiver] == 0), 0, jnp.maximum(room, 0))
    passed = jax.random.randint(jax.random.fold_in(own, 4), (number_of // 2,), 0, 1 << 20) % (room + 1)
    sizes = sizes.at[source_of].add(-passed).at[receiver].add(passed)
    labels = jnp.searchsorted(jnp.cumsum(sizes), jnp.arange(rows * top), side="right").astype(jnp.int32)
    table = labels.reshape(top, rows).T
    table = table[jax.random.permutation(jax.random.fold_in(own, 1), rows)]
    rotation = jax.random.randint(jax.random.fold_in(own, 2), (rows, 1), 0, top)
    return jnp.take_along_axis(table, (jnp.arange(top)[None, :] + rotation) % top, axis=1)


def load_shares(amount, total, bound, skew, full):
    loads = [(1 << 20) // math.isqrt(rank ** skew) + 1 for rank in range(1, amount + 1)]
    largest = bound if full else min(bound, max(-(-total // amount), total * loads[0] // sum(loads)))
    least = 1 if total - largest >= amount - 1 else 0
    holding, spare = [largest] + [least] * (amount - 1), total - largest - least * (amount - 1)
    while spare > 0:
        candidates = [i for i in range(1, amount) if holding[i] < largest] or [i for i in range(1, amount) if holding[i] < bound]
        whole, left = sum([loads[i] for i in candidates]), spare
        for i in candidates:
            addition = min(bound - holding[i], max(1, left * loads[i] // whole), spare)
            holding[i] = holding[i] + addition
            spare = spare - addition
    return np.array(holding)


def centred(stream_key, dims, scale, limit, shards=(), kind=jnp.bfloat16):
    array = scale * jax.random.normal(stream_key, dims, jnp.float32)
    if shards:
        array = array * levels(stream_key, dims, shards, -0.22, 0.18)
    return jnp.clip(array, -limit, limit).astype(kind)


def setup_inputs(seed: int = 0) -> dict:
    splits = jax.random.split(jax.random.key(seed), 8)
    state_field = centred(splits[0], (LEV, NY, NX), 1.0, 6.0, ((1, 16), (2, 2)), jnp.float32)
    diffusion = jnp.clip(jnp.exp(jax.random.uniform(splits[1], (LEV,), jnp.float32, math.log(0.03), math.log(0.24))), 0.03, 0.24)
    weight_in = centred(splits[2], (LEV, HID), LEV ** -0.5, 0.5, (), jnp.float32)
    weight_mid = centred(splits[3], (HID, HID), HID ** -0.5, 0.1875, (), jnp.float32)
    weight_out = centred(splits[4], (HID, LEV), HID ** -0.5, 0.1875, (), jnp.float32)
    block_tile_keys = jax.random.split(jax.random.fold_in(splits[5], 1), REQ // SAMPLES)
    block_tile_turns = jax.random.permutation(jax.random.fold_in(splits[5], 3), REQ // SAMPLES)
    block_tile = jax.vmap(lambda own, number: deal_out(jax.random.fold_in(splits[5], 2), own, number, SAMPLES, N_SIM, 1, 1, 2))(block_tile_keys, block_tile_turns).reshape((REQ, 1))
    block_pos = place_ends(jax.random.randint(splits[6], (REQ,), 0, RY * (RX // BW)), jax.random.fold_in(splits[6], 1), 0, (RY * (RX // BW)) - 1).astype(jnp.int32)
    return dict(state_field=state_field, diffusion=diffusion, weight_in=weight_in, weight_mid=weight_mid, weight_out=weight_out, block_tile=block_tile, block_pos=block_pos)


RATE = 0.5
TARGET_GAIN = 4.0


def diffuse_once(field, diffusion):
    beside_all = jnp.roll(field, 1, 1) + jnp.roll(field, -1, 1)
    beside_all = beside_all + jnp.roll(field, 1, 2) + jnp.roll(field, -1, 2)
    return field + diffusion[:, None, None] * (beside_all - 4.0 * field)


def silu_slope(value):
    sigma = jax.nn.sigmoid(value)
    return sigma * (1.0 + value * (1.0 - sigma))


def gradients(inputs, targets, weight_in, weight_mid, weight_out, count):
    first = weight_in.astype(jnp.bfloat16)
    second = weight_mid.astype(jnp.bfloat16)
    third = weight_out.astype(jnp.bfloat16)
    pre_one = jnp.dot(inputs, first, preferred_element_type=jnp.float32)
    act_one = jax.nn.silu(pre_one).astype(jnp.bfloat16)
    pre_two = jnp.dot(act_one, second, preferred_element_type=jnp.float32)
    act_two = jax.nn.silu(pre_two).astype(jnp.bfloat16)
    output = jnp.dot(act_two, third, preferred_element_type=jnp.float32)
    error = ((output - targets.astype(jnp.float32)) / count).astype(jnp.bfloat16)
    grad_out = jnp.dot(act_two.T, error, preferred_element_type=jnp.float32)
    back_two = jnp.dot(error, third.T, preferred_element_type=jnp.float32)
    delta_two = (back_two * silu_slope(pre_two)).astype(jnp.bfloat16)
    grad_mid = jnp.dot(act_one.T, delta_two, preferred_element_type=jnp.float32)
    back_one = jnp.dot(delta_two, second.T, preferred_element_type=jnp.float32)
    delta_one = (back_one * silu_slope(pre_one)).astype(jnp.bfloat16)
    grad_in = jnp.dot(inputs.T, delta_one, preferred_element_type=jnp.float32)
    return grad_in, grad_mid, grad_out


def reference(state_field, diffusion, weight_in, weight_mid, weight_out, block_tile, block_pos):
    after = diffuse_once(diffuse_once(state_field, diffusion), diffusion)
    increment = after - state_field
    per_row = RX // BW
    total = block_tile.shape[0]
    request = jnp.arange(total, dtype=jnp.int32)
    learner = request // (N_SIM * SAMPLES)
    owner = block_tile[:, 0].astype(jnp.int32)
    places = block_pos.astype(jnp.int32)
    row_start = (owner * RY + places // per_row).astype(jnp.int32)
    col_start = (learner * RX + (places % per_row) * BW).astype(jnp.int32)

    def cut(row, start):
        zero = jnp.zeros((), jnp.int32)
        piece_in = lax.dynamic_slice(state_field, (zero, row, start), (LEV, 1, BW))[:, 0, :]
        piece_target = lax.dynamic_slice(increment, (zero, row, start), (LEV, 1, BW))[:, 0, :]
        return piece_in, piece_target

    cols_in, cols_target = jax.vmap(cut)(row_start, col_start)
    inputs = jnp.swapaxes(cols_in, 1, 2).astype(jnp.bfloat16)
    targets = (TARGET_GAIN * jnp.swapaxes(cols_target, 1, 2)).astype(jnp.bfloat16)
    groups = total // SAMPLES
    inputs = inputs.reshape(groups, SAMPLES * BW, LEV)
    targets = targets.reshape(groups, SAMPLES * BW, LEV)
    count = float(total * BW)

    def accumulate(carry, pair):
        terms = gradients(pair[0], pair[1], weight_in, weight_mid, weight_out, count)
        return tuple(c + t for c, t in zip(carry, terms)), None

    start = (jnp.zeros((LEV, HID), jnp.float32), jnp.zeros((HID, HID), jnp.float32), jnp.zeros((HID, LEV), jnp.float32))
    sums, _ = lax.scan(accumulate, start, (inputs, targets))
    return (after, weight_in - RATE * sums[0], weight_mid - RATE * sums[1], weight_out - RATE * sums[2])
```

```python
import jax
import jax.numpy as jnp
from jax import lax
from jax.experimental import pallas as pl
from jax.experimental.pallas import tpu as pltpu
from jax.sharding import PartitionSpec as P
import functools

BW = 128


RATE = 0.5
TARGET_GAIN = 4.0


def with_halo(x, sides, width):
    for axis, dim in sides:
        size, length = (lax.axis_size(axis), x.shape[dim])
        up = [(i, (i + 1) % size) for i in range(size)]
        down = [(j, i) for i, j in up]
        last = lax.slice_in_dim(x, length - width, length, axis=dim)
        first = lax.slice_in_dim(x, 0, width, axis=dim)
        before = lax.ppermute(last, axis, up)
        after = lax.ppermute(first, axis, down)
        x = jnp.concatenate([before, x, after], axis=dim)
    return x


def interior_step(padded, diffusion):
    center = padded[:, 1:-1, 1:-1]
    beside_all = padded[:, :-2, 1:-1] + padded[:, 2:, 1:-1]
    beside_all = beside_all + padded[:, 1:-1, :-2] + padded[:, 1:-1, 2:]
    return center + diffusion[:, None, None] * (beside_all - 4.0 * center)


def silu_slope(value):
    sigma = jax.nn.sigmoid(value)
    return sigma * (1.0 + value * (1.0 - sigma))


def gradients(inputs, targets, weight_in, weight_mid, weight_out, count):
    first = weight_in.astype(jnp.bfloat16)
    second = weight_mid.astype(jnp.bfloat16)
    third = weight_out.astype(jnp.bfloat16)
    pre_one = jnp.dot(inputs, first, preferred_element_type=jnp.float32)
    act_one = jax.nn.silu(pre_one).astype(jnp.bfloat16)
    pre_two = jnp.dot(act_one, second, preferred_element_type=jnp.float32)
    act_two = jax.nn.silu(pre_two).astype(jnp.bfloat16)
    output = jnp.dot(act_two, third, preferred_element_type=jnp.float32)
    error = ((output - targets.astype(jnp.float32)) / count).astype(jnp.bfloat16)
    grad_out = jnp.dot(error.T, act_two, preferred_element_type=jnp.float32)
    back_two = jnp.dot(error, third.T, preferred_element_type=jnp.float32)
    delta_two = (back_two * silu_slope(pre_two)).astype(jnp.bfloat16)
    grad_mid = jnp.dot(act_one.T, delta_two, preferred_element_type=jnp.float32)
    back_one = jnp.dot(delta_two, second.T, preferred_element_type=jnp.float32)
    delta_one = (back_one * silu_slope(pre_one)).astype(jnp.bfloat16)
    grad_in = jnp.dot(inputs.T, delta_one, preferred_element_type=jnp.float32)
    return (grad_in, grad_mid, grad_out)


MESH = pl.DeviceIdType.MESH


def total_kernel(sizes, parts, rows, cols, *refs):
    seg_refs = refs[: len(rows)]
    out, acc, pair_recv, recv = refs[len(rows) : len(rows) + 4]
    pair_send_sem, pair_recv_sem, rs_send, rs_recv, ag_send, ag_recv, fw_send, fw_recv = refs[
        len(rows) + 4 :
    ]
    sim_size, learn_size = sizes
    sim, learn = lax.axis_index("sim"), lax.axis_index("learn")
    bits = []
    for step in range(sim_size.bit_length() - 1):
        bits.append((lax.rem(sim // (1 << step), 2), 1 << step, 0))
    for step in range(1, learn_size.bit_length() - 1):
        bits.append((lax.rem(learn // (1 << step), 2), 0, 1 << step))
    count = len(bits)
    core = lax.rem(learn, 2)
    other = (sim, learn + 1 - 2 * core)
    partners = [(sim + (1 - 2 * b) * ds, learn + (1 - 2 * b) * dl) for b, ds, dl in bits]

    barrier = pltpu.get_barrier_semaphore()
    for partner in partners + [other]:
        pl.semaphore_signal(barrier, inc=1, device_id=partner, device_id_type=MESH)
    pl.semaphore_wait(barrier, count + 1)

    total_rows = sum(rows)
    half = cols // 2
    width = half // parts
    starts = [sum(rows[:i]) for i in range(len(rows))]

    def column(side, part):
        return pl.multiple_of(side * half + part * width, 128)

    def remote(src, dst, send, recv_, device):
        return pltpu.make_async_remote_copy(
            src_ref=src,
            dst_ref=dst,
            send_sem=send,
            recv_sem=recv_,
            device_id=device,
            device_id_type=MESH,
        )

    pending = []
    pair = {}
    for part in range(parts):
        for i, ref in enumerate(seg_refs):
            copy = remote(
                ref.at[:, pl.ds(column(1 - core, part), width)],
                pair_recv.at[pl.ds(starts[i], rows[i]), pl.ds(part * width, width)],
                pair_send_sem.at[part, i],
                pair_recv_sem.at[part, i],
                other,
            )
            copy.start()
            pair[part, i] = copy
            pending.append(copy)

    region = [(0, total_rows, 0, width) for _ in range(parts)]
    rn_before, left = [], total_rows
    for _ in range(count):
        rn_before.append(left)
        left = left // 2 if (left // 2) % 8 == 0 else left
    sent = [[] for _ in range(parts)]

    def rows_ds(r0, rn):
        return pl.ds(r0 if isinstance(r0, int) else pl.multiple_of(r0, 8), rn)

    def cols_ds(side, part, c0, cn):
        return pl.ds(pl.multiple_of(side * half + part * width + c0, 128), cn)

    def local_ds(part, c0, cn):
        start = part * width + c0
        return pl.ds(start if isinstance(start, int) else pl.multiple_of(start, 128), cn)

    inflight = {}

    def send_half(part, step):
        r0, rn, c0, cn = region[part]
        index = (part + step) % count
        bit = bits[index][0]
        if (rn // 2) % 8 == 0:
            keep = (r0 + bit * (rn // 2), rn // 2, c0, cn)
            give = (r0 + (1 - bit) * (rn // 2), rn // 2, c0, cn)
        else:
            keep = (r0, rn, c0 + bit * (cn // 2), cn // 2)
            give = (r0, rn, c0 + (1 - bit) * (cn // 2), cn // 2)
        offset = sum(r if (r // 2) % 8 else r // 2 for r in rn_before[:step])
        slot = recv.at[pl.ds(offset, keep[1]), pl.ds(part * width, keep[3])]
        copy = remote(
            acc.at[rows_ds(give[0], give[1]), local_ds(part, give[2], give[3])],
            slot,
            rs_send.at[part, step],
            rs_recv.at[part, step],
            partners[index],
        )
        copy.start()
        inflight[part, step] = (copy, slot)
        region[part] = keep
        sent[part].append(index)
        pending.append(copy)

    for part in range(parts):
        for i, ref in enumerate(seg_refs):
            pair[part, i].wait_recv()
            spot = (pl.ds(starts[i], rows[i]), pl.ds(part * width, width))
            acc[spot] = ref[:, pl.ds(column(core, part), width)] + pair_recv[spot]
        send_half(part, 0)

    gathers = {}

    def send_whole(part, step):
        r0, rn, c0, cn = region[part]
        spot = out.at[rows_ds(r0, rn), cols_ds(core, part, c0, cn)]
        copy = remote(
            spot, spot, ag_send.at[part, step], ag_recv.at[part, step], partners[sent[part][step]]
        )
        copy.start()
        gathers[part, step] = copy
        pending.append(copy)

    def forward(part, step, r0, rn, c0, cn):
        spot = out.at[rows_ds(r0, rn), cols_ds(core, part, c0, cn)]
        copy = remote(spot, spot, fw_send.at[part, step], fw_recv.at[part, step], other)
        copy.start()
        forwards.append(copy)

    forwards = []
    for step in range(count):
        for part in range(parts):
            copy, slot = inflight[part, step]
            copy.wait_recv()
            r0, rn, c0, cn = region[part]
            spot = (rows_ds(r0, rn), local_ds(part, c0, cn))
            if step < count - 1:
                acc[spot] += slot[...]
                send_half(part, step + 1)
            else:
                out[rows_ds(r0, rn), cols_ds(core, part, c0, cn)] = acc[spot] + slot[...]
                send_whole(part, step)
                forward(part, count, r0, rn, c0, cn)

    for step in reversed(range(count)):
        for part in range(parts):
            gathers[part, step].wait_recv()
            r0, rn, c0, cn = region[part]
            bit = bits[sent[part][step]][0]
            if (rn_before[step]) == rn:
                got = (r0, rn, c0 + (1 - 2 * bit) * cn, cn)
                region[part] = (r0, rn, c0 - bit * cn, 2 * cn)
            else:
                got = (r0 + (1 - 2 * bit) * rn, rn, c0, cn)
                region[part] = (r0 - bit * rn, 2 * rn, c0, cn)
            if step > 0:
                send_whole(part, step - 1)
            forward(part, step, *got)

    for copy in pending:
        copy.wait_send()
    for copy in forwards:
        copy.wait()


def total(sizes, segments):
    rows = tuple(s.shape[0] for s in segments)
    cols = segments[0].shape[1]
    count = sizes[0].bit_length() - 1 + sizes[1].bit_length() - 2
    total_rows = sum(rows)
    parts = 4 if (total_rows >> count) % 8 == 0 else 2
    vmem = pl.BlockSpec(memory_space=pltpu.VMEM)
    dma = lambda *shape: pltpu.SemaphoreType.DMA(shape)
    result = pl.pallas_call(
        functools.partial(total_kernel, sizes, parts, rows, cols),
        out_shape=jax.ShapeDtypeStruct((total_rows, cols), jnp.float32),
        in_specs=[vmem] * len(rows),
        out_specs=vmem,
        scratch_shapes=[
            pltpu.VMEM((total_rows, cols // 2), jnp.float32),
            pltpu.VMEM((total_rows, cols // 2), jnp.float32),
            pltpu.VMEM((total_rows + 64, cols // 2), jnp.float32),
            dma(parts, len(rows)),
            dma(parts, len(rows)),
            dma(parts, count),
            dma(parts, count),
            dma(parts, count),
            dma(parts, count),
            dma(parts, count + 1),
            dma(parts, count + 1),
        ],
        compiler_params=pltpu.CompilerParams(
            collective_id=0, has_side_effects=True, vmem_limit_bytes=48 << 20
        ),
    )(*segments)
    at = 0
    outs = []
    for r in rows:
        outs.append(result[at : at + r])
        at += r
    return outs


def on_device(state_field, diffusion, weight_in, weight_mid, weight_out, block_tile, block_pos):
    levels, tile_rows, tile_cols = state_field.shape
    padded = with_halo(state_field, (("sim", 1), ("learn", 2)), 2)
    after = interior_step(interior_step(padded, diffusion), diffusion)
    increment = after - state_field
    senders = lax.axis_size("sim")
    own_index = lax.axis_index("sim")
    samples = block_tile.shape[0] // senders
    per_row = tile_cols // BW
    tiles = block_tile[:, 0].reshape(senders, samples)
    places = block_pos.reshape(senders, samples)
    matched = tiles == own_index
    place = jnp.sum(jnp.where(matched, places, 0), axis=1)
    present = jnp.any(matched, axis=1)

    def cut(spot):
        row = spot // per_row
        start = spot % per_row * BW
        zero = jnp.zeros((), jnp.int32)
        piece_in = lax.dynamic_slice(state_field, (zero, row, start), (levels, 1, BW))[:, 0, :]
        piece_target = lax.dynamic_slice(increment, (zero, row, start), (levels, 1, BW))[:, 0, :]
        return (piece_in, piece_target)

    cols_in, cols_target = jax.vmap(cut)(place)
    keep = present[:, None, None]
    send_in = jnp.where(keep, jnp.swapaxes(cols_in, 1, 2), 0.0).astype(jnp.bfloat16)
    send_target = jnp.where(keep, TARGET_GAIN * jnp.swapaxes(cols_target, 1, 2), 0.0).astype(
        jnp.bfloat16
    )
    got_in, got_target = (
        lax.all_to_all(send_in, "sim", split_axis=0, concat_axis=0, tiled=True),
        lax.all_to_all(send_target, "sim", split_axis=0, concat_axis=0, tiled=True),
    )
    wanted = lax.dynamic_slice_in_dim(tiles, own_index, 1, 0)[0]
    inputs = jnp.take(got_in, wanted, axis=0).reshape(-1, levels)
    targets = jnp.take(got_target, wanted, axis=0).reshape(-1, levels)
    count = float(senders * lax.axis_size("learn") * samples * BW)
    grad_in, grad_mid, grad_out = gradients(
        inputs, targets, weight_in, weight_mid, weight_out, count
    )
    sizes = (senders, lax.axis_size("learn"))
    total_in, total_mid, total_out = total(sizes, (grad_in, grad_mid, grad_out))
    new_in = weight_in - RATE * total_in
    new_mid = weight_mid - RATE * total_mid
    new_out = weight_out - RATE * total_out.T
    return (after, new_in, new_mid, new_out)


def solution(mesh):
    placed = (P(None, "sim", "learn"), P(), P(), P(), P(), P("learn", None), P("learn"))
    return jax.shard_map(
        on_device,
        mesh=mesh,
        in_specs=placed,
        out_specs=(P(None, "sim", "learn"), P(), P(), P()),
        check_vma=False,
    )
```

```python
import jax
import jax.numpy as jnp
from jax import lax
from jax.experimental import pallas as pl
from jax.experimental.pallas import tpu as pltpu
from jax.sharding import PartitionSpec as P
import functools

BW = 128


RATE = 0.5
TARGET_GAIN = 4.0


def with_halo(x, sides, width):
    for axis, dim in sides:
        size, length = (lax.axis_size(axis), x.shape[dim])
        up = [(i, (i + 1) % size) for i in range(size)]
        down = [(j, i) for i, j in up]
        last = lax.slice_in_dim(x, length - width, length, axis=dim)
        first = lax.slice_in_dim(x, 0, width, axis=dim)
        before = lax.ppermute(last, axis, up)
        after = lax.ppermute(first, axis, down)
        x = jnp.concatenate([before, x, after], axis=dim)
    return x


def interior_step(padded, diffusion):
    center = padded[:, 1:-1, 1:-1]
    beside_all = padded[:, :-2, 1:-1] + padded[:, 2:, 1:-1]
    beside_all = beside_all + padded[:, 1:-1, :-2] + padded[:, 1:-1, 2:]
    return center + diffusion[:, None, None] * (beside_all - 4.0 * center)


def silu_slope(value):
    sigma = jax.nn.sigmoid(value)
    return sigma * (1.0 + value * (1.0 - sigma))


def gradients(inputs, targets, weight_in, weight_mid, weight_out, count):
    first = weight_in.astype(jnp.bfloat16)
    second = weight_mid.astype(jnp.bfloat16)
    third = weight_out.astype(jnp.bfloat16)
    pre_one = jnp.dot(inputs, first, preferred_element_type=jnp.float32)
    act_one = jax.nn.silu(pre_one).astype(jnp.bfloat16)
    pre_two = jnp.dot(act_one, second, preferred_element_type=jnp.float32)
    act_two = jax.nn.silu(pre_two).astype(jnp.bfloat16)
    output = jnp.dot(act_two, third, preferred_element_type=jnp.float32)
    error = ((output - targets.astype(jnp.float32)) / count).astype(jnp.bfloat16)
    grad_out = jnp.dot(error.T, act_two, preferred_element_type=jnp.float32)
    back_two = jnp.dot(error, third.T, preferred_element_type=jnp.float32)
    delta_two = (back_two * silu_slope(pre_two)).astype(jnp.bfloat16)
    grad_mid = jnp.dot(act_one.T, delta_two, preferred_element_type=jnp.float32)
    back_one = jnp.dot(delta_two, second.T, preferred_element_type=jnp.float32)
    delta_one = (back_one * silu_slope(pre_one)).astype(jnp.bfloat16)
    grad_in = jnp.dot(inputs.T, delta_one, preferred_element_type=jnp.float32)
    return (grad_in, grad_mid, grad_out)


MESH = pl.DeviceIdType.MESH


def total_kernel(sizes, parts, rows, cols, *refs):
    seg_refs = refs[: len(rows)]
    out, acc, pair_recv, recv = refs[len(rows) : len(rows) + 4]
    pair_send_sem, pair_recv_sem, rs_send, rs_recv, ag_send, ag_recv, fw_send, fw_recv = refs[
        len(rows) + 4 :
    ]
    sim_size, learn_size = sizes
    sim, learn = lax.axis_index("sim"), lax.axis_index("learn")
    bits = []
    for step in range(sim_size.bit_length() - 1):
        bits.append((lax.rem(sim // (1 << step), 2), 1 << step, 0))
    for step in range(1, learn_size.bit_length() - 1):
        bits.append((lax.rem(learn // (1 << step), 2), 0, 1 << step))
    count = len(bits)
    core = lax.rem(learn, 2)
    other = (sim, learn + 1 - 2 * core)
    partners = [(sim + (1 - 2 * b) * ds, learn + (1 - 2 * b) * dl) for b, ds, dl in bits]

    barrier = pltpu.get_barrier_semaphore()
    for partner in partners + [other]:
        pl.semaphore_signal(barrier, inc=1, device_id=partner, device_id_type=MESH)
    pl.semaphore_wait(barrier, count + 1)

    total_rows = sum(rows)
    half = cols // 2
    width = half // parts
    starts = [sum(rows[:i]) for i in range(len(rows))]

    def column(side, part):
        return pl.multiple_of(side * half + part * width, 128)

    def remote(src, dst, send, recv_, device):
        return pltpu.make_async_remote_copy(
            src_ref=src,
            dst_ref=dst,
            send_sem=send,
            recv_sem=recv_,
            device_id=device,
            device_id_type=MESH,
        )

    pending = []
    pair = {}
    for part in range(parts):
        for i, ref in enumerate(seg_refs):
            copy = remote(
                ref.at[:, pl.ds(column(1 - core, part), width)],
                pair_recv.at[pl.ds(starts[i], rows[i]), pl.ds(part * width, width)],
                pair_send_sem.at[part, i],
                pair_recv_sem.at[part, i],
                other,
            )
            copy.start()
            pair[part, i] = copy
            pending.append(copy)

    region = [(0, total_rows, 0, width) for _ in range(parts)]
    rn_before, left = [], total_rows
    for _ in range(count):
        rn_before.append(left)
        left = left // 2 if (left // 2) % 8 == 0 else left
    sent = [[] for _ in range(parts)]

    def rows_ds(r0, rn):
        return pl.ds(r0 if isinstance(r0, int) else pl.multiple_of(r0, 8), rn)

    def cols_ds(side, part, c0, cn):
        return pl.ds(pl.multiple_of(side * half + part * width + c0, 128), cn)

    def local_ds(part, c0, cn):
        start = part * width + c0
        return pl.ds(start if isinstance(start, int) else pl.multiple_of(start, 128), cn)

    inflight = {}

    def send_half(part, step):
        r0, rn, c0, cn = region[part]
        index = (part + step) % count
        bit = bits[index][0]
        if (rn // 2) % 8 == 0:
            keep = (r0 + bit * (rn // 2), rn // 2, c0, cn)
            give = (r0 + (1 - bit) * (rn // 2), rn // 2, c0, cn)
        else:
            keep = (r0, rn, c0 + bit * (cn // 2), cn // 2)
            give = (r0, rn, c0 + (1 - bit) * (cn // 2), cn // 2)
        offset = sum(r if (r // 2) % 8 else r // 2 for r in rn_before[:step])
        slot = recv.at[pl.ds(offset, keep[1]), pl.ds(part * width, keep[3])]
        copy = remote(
            acc.at[rows_ds(give[0], give[1]), local_ds(part, give[2], give[3])],
            slot,
            rs_send.at[part, step],
            rs_recv.at[part, step],
            partners[index],
        )
        copy.start()
        inflight[part, step] = (copy, slot)
        region[part] = keep
        sent[part].append(index)
        pending.append(copy)

    for part in range(parts):
        for i, ref in enumerate(seg_refs):
            pair[part, i].wait_recv()
            spot = (pl.ds(starts[i], rows[i]), pl.ds(part * width, width))
            acc[spot] = ref[:, pl.ds(column(core, part), width)] + pair_recv[spot]
        send_half(part, 0)

    gathers = {}

    def send_whole(part, step):
        r0, rn, c0, cn = region[part]
        spot = out.at[rows_ds(r0, rn), cols_ds(core, part, c0, cn)]
        copy = remote(
            spot, spot, ag_send.at[part, step], ag_recv.at[part, step], partners[sent[part][step]]
        )
        copy.start()
        gathers[part, step] = copy
        pending.append(copy)

    def forward(part, step, r0, rn, c0, cn):
        spot = out.at[rows_ds(r0, rn), cols_ds(core, part, c0, cn)]
        copy = remote(spot, spot, fw_send.at[part, step], fw_recv.at[part, step], other)
        copy.start()
        forwards.append(copy)

    forwards = []
    for step in range(count):
        for part in range(parts):
            copy, slot = inflight[part, step]
            copy.wait_recv()
            r0, rn, c0, cn = region[part]
            spot = (rows_ds(r0, rn), local_ds(part, c0, cn))
            if step < count - 1:
                acc[spot] += slot[...]
                send_half(part, step + 1)
            else:
                out[rows_ds(r0, rn), cols_ds(core, part, c0, cn)] = acc[spot] + slot[...]
                send_whole(part, step)
                forward(part, count, r0, rn, c0, cn)

    for step in reversed(range(count)):
        for part in range(parts):
            gathers[part, step].wait_recv()
            r0, rn, c0, cn = region[part]
            bit = bits[sent[part][step]][0]
            if (rn_before[step]) == rn:
                got = (r0, rn, c0 + (1 - 2 * bit) * cn, cn)
                region[part] = (r0, rn, c0 - bit * cn, 2 * cn)
            else:
                got = (r0 + (1 - 2 * bit) * rn, rn, c0, cn)
                region[part] = (r0 - bit * rn, 2 * rn, c0, cn)
            if step > 0:
                send_whole(part, step - 1)
            forward(part, step, *got)

    for copy in pending:
        copy.wait_send()
    for copy in forwards:
        copy.wait()


def total(sizes, segments):
    rows = tuple(s.shape[0] for s in segments)
    cols = segments[0].shape[1]
    count = sizes[0].bit_length() - 1 + sizes[1].bit_length() - 2
    total_rows = sum(rows)
    parts = 4 if (total_rows >> count) % 8 == 0 else 2
    vmem = pl.BlockSpec(memory_space=pltpu.VMEM)
    dma = lambda *shape: pltpu.SemaphoreType.DMA(shape)
    result = pl.pallas_call(
        functools.partial(total_kernel, sizes, parts, rows, cols),
        out_shape=jax.ShapeDtypeStruct((total_rows, cols), jnp.float32),
        in_specs=[vmem] * len(rows),
        out_specs=vmem,
        scratch_shapes=[
            pltpu.VMEM((total_rows, cols // 2), jnp.float32),
            pltpu.VMEM((total_rows, cols // 2), jnp.float32),
            pltpu.VMEM((total_rows + 64, cols // 2), jnp.float32),
            dma(parts, len(rows)),
            dma(parts, len(rows)),
            dma(parts, count),
            dma(parts, count),
            dma(parts, count),
            dma(parts, count),
            dma(parts, count + 1),
            dma(parts, count + 1),
        ],
        compiler_params=pltpu.CompilerParams(
            collective_id=0, has_side_effects=True, vmem_limit_bytes=48 << 20
        ),
    )(*segments)
    at = 0
    outs = []
    for r in rows:
        outs.append(result[at : at + r])
        at += r
    return outs


def on_device(state_field, diffusion, weight_in, weight_mid, weight_out, block_tile, block_pos):
    levels, tile_rows, tile_cols = state_field.shape
    padded = with_halo(state_field, (("sim", 1), ("learn", 2)), 2)
    after = interior_step(interior_step(padded, diffusion), diffusion)
    increment = after - state_field
    senders = lax.axis_size("sim")
    own_index = lax.axis_index("sim")
    samples = block_tile.shape[0] // senders
    per_row = tile_cols // BW
    tiles = block_tile[:, 0].reshape(senders, samples)
    places = block_pos.reshape(senders, samples)
    matched = tiles == own_index
    place = jnp.sum(jnp.where(matched, places, 0), axis=1)
    present = jnp.any(matched, axis=1)

    def cut(spot):
        row = spot // per_row
        start = spot % per_row * BW
        zero = jnp.zeros((), jnp.int32)
        piece_in = lax.dynamic_slice(state_field, (zero, row, start), (levels, 1, BW))[:, 0, :]
        piece_target = lax.dynamic_slice(increment, (zero, row, start), (levels, 1, BW))[:, 0, :]
        return (piece_in, piece_target)

    cols_in, cols_target = jax.vmap(cut)(place)
    keep = present[:, None, None]
    send_in = jnp.where(keep, jnp.swapaxes(cols_in, 1, 2), 0.0).astype(jnp.bfloat16)
    send_target = jnp.where(keep, TARGET_GAIN * jnp.swapaxes(cols_target, 1, 2), 0.0).astype(
        jnp.bfloat16
    )
    inputs = send_in.reshape(-1, levels)
    targets = send_target.reshape(-1, levels)
    count = float(senders * lax.axis_size("learn") * samples * BW)
    grad_in, grad_mid, grad_out = gradients(
        inputs, targets, weight_in, weight_mid, weight_out, count
    )
    sizes = (senders, lax.axis_size("learn"))
    total_in, total_mid, total_out = total(sizes, (grad_in, grad_mid, grad_out))
    new_in = weight_in - RATE * total_in
    new_mid = weight_mid - RATE * total_mid
    new_out = weight_out - RATE * total_out.T
    return (after, new_in, new_mid, new_out)


def solution(mesh):
    placed = (P(None, "sim", "learn"), P(), P(), P(), P(), P("learn", None), P("learn"))
    return jax.shard_map(
        on_device,
        mesh=mesh,
        in_specs=placed,
        out_specs=(P(None, "sim", "learn"), P(), P(), P()),
        check_vma=False,
    )
```

```python
import jax
import jax.numpy as jnp
from jax import lax
from jax.experimental import pallas as pl
from jax.experimental.pallas import tpu as pltpu
from jax.sharding import PartitionSpec as P
import functools

BW = 128


RATE = 0.5
TARGET_GAIN = 4.0


def with_halo(x, sides, width):
    for axis, dim in sides:
        size, length = (lax.axis_size(axis), x.shape[dim])
        up = [(i, (i + 1) % size) for i in range(size)]
        down = [(j, i) for i, j in up]
        last = lax.slice_in_dim(x, length - width, length, axis=dim)
        first = lax.slice_in_dim(x, 0, width, axis=dim)
        before = lax.ppermute(last, axis, up)
        after = lax.ppermute(first, axis, down)
        x = jnp.concatenate([before, x, after], axis=dim)
    return x


def interior_step(padded, diffusion):
    center = padded[:, 1:-1, 1:-1]
    beside_all = padded[:, :-2, 1:-1] + padded[:, 2:, 1:-1]
    beside_all = beside_all + padded[:, 1:-1, :-2] + padded[:, 1:-1, 2:]
    return center + diffusion[:, None, None] * (beside_all - 4.0 * center)


def silu_slope(value):
    sigma = jax.nn.sigmoid(value)
    return sigma * (1.0 + value * (1.0 - sigma))


def gradients(inputs, targets, weight_in, weight_mid, weight_out, count):
    first = weight_in.astype(jnp.bfloat16)
    second = weight_mid.astype(jnp.bfloat16)
    third = weight_out.astype(jnp.bfloat16)
    pre_one = jnp.dot(inputs, first, preferred_element_type=jnp.float32)
    act_one = jax.nn.silu(pre_one).astype(jnp.bfloat16)
    pre_two = jnp.dot(act_one, second, preferred_element_type=jnp.float32)
    act_two = jax.nn.silu(pre_two).astype(jnp.bfloat16)
    output = jnp.dot(act_two, third, preferred_element_type=jnp.float32)
    error = ((output - targets.astype(jnp.float32)) / count).astype(jnp.bfloat16)
    grad_out = jnp.dot(error.T, act_two, preferred_element_type=jnp.float32)
    back_two = jnp.dot(error, third.T, preferred_element_type=jnp.float32)
    delta_two = (back_two * silu_slope(pre_two)).astype(jnp.bfloat16)
    grad_mid = jnp.dot(act_one.T, delta_two, preferred_element_type=jnp.float32)
    back_one = jnp.dot(delta_two, second.T, preferred_element_type=jnp.float32)
    delta_one = (back_one * silu_slope(pre_one)).astype(jnp.bfloat16)
    grad_in = jnp.dot(inputs.T, delta_one, preferred_element_type=jnp.float32)
    return (grad_in, grad_mid, grad_out)


MESH = pl.DeviceIdType.MESH


def total_kernel(sizes, parts, rows, cols, *refs):
    seg_refs = refs[: len(rows)]
    out, acc, pair_recv, recv = refs[len(rows) : len(rows) + 4]
    pair_send_sem, pair_recv_sem, rs_send, rs_recv, ag_send, ag_recv, fw_send, fw_recv = refs[
        len(rows) + 4 :
    ]
    sim_size, learn_size = sizes
    sim, learn = lax.axis_index("sim"), lax.axis_index("learn")
    bits = []
    for step in range(sim_size.bit_length() - 1):
        bits.append((lax.rem(sim // (1 << step), 2), 1 << step, 0))
    for step in range(1, learn_size.bit_length() - 1):
        bits.append((lax.rem(learn // (1 << step), 2), 0, 1 << step))
    count = len(bits)
    near = min(3, count)
    core = lax.rem(learn, 2)
    other = (sim, learn + 1 - 2 * core)
    partners = [(sim + (1 - 2 * b) * ds, learn + (1 - 2 * b) * dl) for b, ds, dl in bits]

    barrier = pltpu.get_barrier_semaphore()
    for partner in partners + [other]:
        pl.semaphore_signal(barrier, inc=1, device_id=partner, device_id_type=MESH)
    pl.semaphore_wait(barrier, count + 1)

    total_rows = sum(rows)
    half = cols // 2
    width = half // parts
    starts = [sum(rows[:i]) for i in range(len(rows))]

    def column(side, part):
        return pl.multiple_of(side * half + part * width, 128)

    def remote(src, dst, send, recv_, device):
        return pltpu.make_async_remote_copy(
            src_ref=src,
            dst_ref=dst,
            send_sem=send,
            recv_sem=recv_,
            device_id=device,
            device_id_type=MESH,
        )

    pending = []
    pair = {}
    for part in range(parts):
        for i, ref in enumerate(seg_refs):
            copy = remote(
                ref.at[:, pl.ds(column(1 - core, part), width)],
                pair_recv.at[pl.ds(starts[i], rows[i]), pl.ds(part * width, width)],
                pair_send_sem.at[part, i],
                pair_recv_sem.at[part, i],
                other,
            )
            copy.start()
            pair[part, i] = copy
            pending.append(copy)

    region = [(0, total_rows, 0, width) for _ in range(parts)]
    rn_before, left = [], total_rows
    for _ in range(count):
        rn_before.append(left)
        left = left // 2 if (left // 2) % 8 == 0 else left
    sent = [[] for _ in range(parts)]

    def rows_ds(r0, rn):
        return pl.ds(r0 if isinstance(r0, int) else pl.multiple_of(r0, 8), rn)

    def cols_ds(side, part, c0, cn):
        return pl.ds(pl.multiple_of(side * half + part * width + c0, 128), cn)

    def local_ds(part, c0, cn):
        start = part * width + c0
        return pl.ds(start if isinstance(start, int) else pl.multiple_of(start, 128), cn)

    inflight = {}

    def send_half(part, step):
        r0, rn, c0, cn = region[part]
        index = (part + step) % near if step < near else step
        bit = bits[index][0]
        if (rn // 2) % 8 == 0:
            keep = (r0 + bit * (rn // 2), rn // 2, c0, cn)
            give = (r0 + (1 - bit) * (rn // 2), rn // 2, c0, cn)
        else:
            keep = (r0, rn, c0 + bit * (cn // 2), cn // 2)
            give = (r0, rn, c0 + (1 - bit) * (cn // 2), cn // 2)
        offset = sum(r if (r // 2) % 8 else r // 2 for r in rn_before[:step])
        slot = recv.at[pl.ds(offset, keep[1]), pl.ds(part * width, keep[3])]
        copy = remote(
            acc.at[rows_ds(give[0], give[1]), local_ds(part, give[2], give[3])],
            slot,
            rs_send.at[part, step],
            rs_recv.at[part, step],
            partners[index],
        )
        copy.start()
        inflight[part, step] = (copy, slot)
        region[part] = keep
        sent[part].append(index)
        pending.append(copy)

    for part in range(parts):
        for i, ref in enumerate(seg_refs):
            pair[part, i].wait_recv()
            spot = (pl.ds(starts[i], rows[i]), pl.ds(part * width, width))
            acc[spot] = ref[:, pl.ds(column(core, part), width)] + pair_recv[spot]
        send_half(part, 0)

    gathers = {}

    def send_whole(part, step):
        r0, rn, c0, cn = region[part]
        spot = out.at[rows_ds(r0, rn), cols_ds(core, part, c0, cn)]
        copy = remote(
            spot, spot, ag_send.at[part, step], ag_recv.at[part, step], partners[sent[part][step]]
        )
        copy.start()
        gathers[part, step] = copy
        pending.append(copy)

    def forward(part, step, r0, rn, c0, cn):
        spot = out.at[rows_ds(r0, rn), cols_ds(core, part, c0, cn)]
        copy = remote(spot, spot, fw_send.at[part, step], fw_recv.at[part, step], other)
        copy.start()
        forwards.append(copy)

    forwards = []
    for step in range(count):
        for part in range(parts):
            copy, slot = inflight[part, step]
            copy.wait_recv()
            r0, rn, c0, cn = region[part]
            spot = (rows_ds(r0, rn), local_ds(part, c0, cn))
            if step < count - 1:
                acc[spot] += slot[...]
                send_half(part, step + 1)
            else:
                out[rows_ds(r0, rn), cols_ds(core, part, c0, cn)] = acc[spot] + slot[...]
                send_whole(part, step)
                forward(part, count, r0, rn, c0, cn)

    for step in reversed(range(count)):
        for part in range(parts):
            gathers[part, step].wait_recv()
            r0, rn, c0, cn = region[part]
            bit = bits[sent[part][step]][0]
            if (rn_before[step]) == rn:
                got = (r0, rn, c0 + (1 - 2 * bit) * cn, cn)
                region[part] = (r0, rn, c0 - bit * cn, 2 * cn)
            else:
                got = (r0 + (1 - 2 * bit) * rn, rn, c0, cn)
                region[part] = (r0 - bit * rn, 2 * rn, c0, cn)
            if step > 0:
                send_whole(part, step - 1)
            forward(part, step, *got)

    for copy in pending:
        copy.wait_send()
    for copy in forwards:
        copy.wait()


def total(sizes, segments):
    rows = tuple(s.shape[0] for s in segments)
    cols = segments[0].shape[1]
    count = sizes[0].bit_length() - 1 + sizes[1].bit_length() - 2
    total_rows = sum(rows)
    parts = 4 if (total_rows >> count) % 8 == 0 else 2
    vmem = pl.BlockSpec(memory_space=pltpu.VMEM)
    dma = lambda *shape: pltpu.SemaphoreType.DMA(shape)
    result = pl.pallas_call(
        functools.partial(total_kernel, sizes, parts, rows, cols),
        out_shape=jax.ShapeDtypeStruct((total_rows, cols), jnp.float32),
        in_specs=[vmem] * len(rows),
        out_specs=vmem,
        scratch_shapes=[
            pltpu.VMEM((total_rows, cols // 2), jnp.float32),
            pltpu.VMEM((total_rows, cols // 2), jnp.float32),
            pltpu.VMEM((total_rows + 64, cols // 2), jnp.float32),
            dma(parts, len(rows)),
            dma(parts, len(rows)),
            dma(parts, count),
            dma(parts, count),
            dma(parts, count),
            dma(parts, count),
            dma(parts, count + 1),
            dma(parts, count + 1),
        ],
        compiler_params=pltpu.CompilerParams(
            collective_id=0, has_side_effects=True, vmem_limit_bytes=48 << 20
        ),
    )(*segments)
    at = 0
    outs = []
    for r in rows:
        outs.append(result[at : at + r])
        at += r
    return outs


def on_device(state_field, diffusion, weight_in, weight_mid, weight_out, block_tile, block_pos):
    levels, tile_rows, tile_cols = state_field.shape
    padded = with_halo(state_field, (("sim", 1), ("learn", 2)), 2)
    after = interior_step(interior_step(padded, diffusion), diffusion)
    increment = after - state_field
    senders = lax.axis_size("sim")
    own_index = lax.axis_index("sim")
    samples = block_tile.shape[0] // senders
    per_row = tile_cols // BW
    tiles = block_tile[:, 0].reshape(senders, samples)
    places = block_pos.reshape(senders, samples)
    matched = tiles == own_index
    place = jnp.sum(jnp.where(matched, places, 0), axis=1)
    present = jnp.any(matched, axis=1)

    def cut(spot):
        row = spot // per_row
        start = spot % per_row * BW
        zero = jnp.zeros((), jnp.int32)
        piece_in = lax.dynamic_slice(state_field, (zero, row, start), (levels, 1, BW))[:, 0, :]
        piece_target = lax.dynamic_slice(increment, (zero, row, start), (levels, 1, BW))[:, 0, :]
        return (piece_in, piece_target)

    cols_in, cols_target = jax.vmap(cut)(place)
    keep = present[:, None, None]
    send_in = jnp.where(keep, jnp.swapaxes(cols_in, 1, 2), 0.0).astype(jnp.bfloat16)
    send_target = jnp.where(keep, TARGET_GAIN * jnp.swapaxes(cols_target, 1, 2), 0.0).astype(
        jnp.bfloat16
    )
    inputs = send_in.reshape(-1, levels)
    targets = send_target.reshape(-1, levels)
    count = float(senders * lax.axis_size("learn") * samples * BW)
    grad_in, grad_mid, grad_out = gradients(
        inputs, targets, weight_in, weight_mid, weight_out, count
    )
    sizes = (senders, lax.axis_size("learn"))
    total_in, total_mid, total_out = total(sizes, (grad_in, grad_mid, grad_out))
    new_in = weight_in - RATE * total_in
    new_mid = weight_mid - RATE * total_mid
    new_out = weight_out - RATE * total_out.T
    return (after, new_in, new_mid, new_out)


def solution(mesh):
    placed = (P(None, "sim", "learn"), P(), P(), P(), P(), P("learn", None), P("learn"))
    return jax.shard_map(
        on_device,
        mesh=mesh,
        in_specs=placed,
        out_specs=(P(None, "sim", "learn"), P(), P(), P()),
        check_vma=False,
    )
```

```python
import jax
import jax.numpy as jnp
from jax import lax
from jax.experimental import pallas as pl
from jax.experimental.pallas import tpu as pltpu
from jax.sharding import PartitionSpec as P
import functools

BW = 128


RATE = 0.5
TARGET_GAIN = 4.0


def halo(x, axis, dim, width):
    size, length = (lax.axis_size(axis), x.shape[dim])
    up = [(i, (i + 1) % size) for i in range(size)]
    down = [(j, i) for i, j in up]
    last = lax.slice_in_dim(x, length - width, length, axis=dim)
    first = lax.slice_in_dim(x, 0, width, axis=dim)
    before = lax.ppermute(last, axis, up)
    after = lax.ppermute(first, axis, down)
    return before, after


def interior_step(padded, diffusion):
    center = padded[:, 1:-1, 1:-1]
    beside_all = padded[:, :-2, 1:-1] + padded[:, 2:, 1:-1]
    beside_all = beside_all + padded[:, 1:-1, :-2] + padded[:, 1:-1, 2:]
    return center + diffusion[:, None, None] * (beside_all - 4.0 * center)


def silu_slope(value):
    sigma = jax.nn.sigmoid(value)
    return sigma * (1.0 + value * (1.0 - sigma))


def forward(inputs, weight_in, weight_mid):
    first = weight_in.astype(jnp.bfloat16)
    second = weight_mid.astype(jnp.bfloat16)
    pre_one = jnp.dot(inputs, first, preferred_element_type=jnp.float32)
    act_one = jax.nn.silu(pre_one).astype(jnp.bfloat16)
    pre_two = jnp.dot(act_one, second, preferred_element_type=jnp.float32)
    act_two = jax.nn.silu(pre_two).astype(jnp.bfloat16)
    return pre_one, act_one, pre_two, act_two


def gradients(inputs, targets, saved, output, weight_mid, weight_out, count):
    pre_one, act_one, pre_two, act_two = saved
    second = weight_mid.astype(jnp.bfloat16)
    third = weight_out.astype(jnp.bfloat16)
    error = ((output - targets.astype(jnp.float32)) / count).astype(jnp.bfloat16)
    grad_out = jnp.dot(error.T, act_two, preferred_element_type=jnp.float32)
    back_two = jnp.dot(error, third.T, preferred_element_type=jnp.float32)
    delta_two = (back_two * silu_slope(pre_two)).astype(jnp.bfloat16)
    grad_mid = jnp.dot(act_one.T, delta_two, preferred_element_type=jnp.float32)
    back_one = jnp.dot(delta_two, second.T, preferred_element_type=jnp.float32)
    delta_one = (back_one * silu_slope(pre_one)).astype(jnp.bfloat16)
    grad_in = jnp.dot(inputs.T, delta_one, preferred_element_type=jnp.float32)
    return (grad_in, grad_mid, grad_out)


MESH = pl.DeviceIdType.MESH


def total_kernel(sizes, parts, rows, cols, *refs):
    seg_refs = refs[: len(rows)]
    out, acc, pair_recv, recv = refs[len(rows) : len(rows) + 4]
    pair_send_sem, pair_recv_sem, rs_send, rs_recv, ag_send, ag_recv, fw_send, fw_recv = refs[
        len(rows) + 4 :
    ]
    sim_size, learn_size = sizes
    sim, learn = lax.axis_index("sim"), lax.axis_index("learn")
    bits = []
    for step in range(sim_size.bit_length() - 1):
        bits.append((lax.rem(sim // (1 << step), 2), 1 << step, 0))
    for step in range(1, learn_size.bit_length() - 1):
        bits.append((lax.rem(learn // (1 << step), 2), 0, 1 << step))
    count = len(bits)
    near = min(3, count)
    core = lax.rem(learn, 2)
    other = (sim, learn + 1 - 2 * core)
    partners = [(sim + (1 - 2 * b) * ds, learn + (1 - 2 * b) * dl) for b, ds, dl in bits]

    barrier = pltpu.get_barrier_semaphore()
    for partner in partners + [other]:
        pl.semaphore_signal(barrier, inc=1, device_id=partner, device_id_type=MESH)
    pl.semaphore_wait(barrier, count + 1)

    total_rows = sum(rows)
    half = cols // 2
    width = half // parts
    starts = [sum(rows[:i]) for i in range(len(rows))]

    def column(side, part):
        return pl.multiple_of(side * half + part * width, 128)

    def remote(src, dst, send, recv_, device):
        return pltpu.make_async_remote_copy(
            src_ref=src,
            dst_ref=dst,
            send_sem=send,
            recv_sem=recv_,
            device_id=device,
            device_id_type=MESH,
        )

    pending = []
    pair = {}
    for part in range(parts):
        for i, ref in enumerate(seg_refs):
            copy = remote(
                ref.at[:, pl.ds(column(1 - core, part), width)],
                pair_recv.at[pl.ds(starts[i], rows[i]), pl.ds(part * width, width)],
                pair_send_sem.at[part, i],
                pair_recv_sem.at[part, i],
                other,
            )
            copy.start()
            pair[part, i] = copy
            pending.append(copy)

    region = [(0, total_rows, 0, width) for _ in range(parts)]
    rn_before, left = [], total_rows
    for _ in range(count):
        rn_before.append(left)
        left = left // 2 if (left // 2) % 8 == 0 else left
    sent = [[] for _ in range(parts)]

    def rows_ds(r0, rn):
        return pl.ds(r0 if isinstance(r0, int) else pl.multiple_of(r0, 8), rn)

    def cols_ds(side, part, c0, cn):
        return pl.ds(pl.multiple_of(side * half + part * width + c0, 128), cn)

    def local_ds(part, c0, cn):
        start = part * width + c0
        return pl.ds(start if isinstance(start, int) else pl.multiple_of(start, 128), cn)

    inflight = {}

    def send_half(part, step):
        r0, rn, c0, cn = region[part]
        index = (part + step) % near if step < near else step
        bit = bits[index][0]
        if (rn // 2) % 8 == 0:
            keep = (r0 + bit * (rn // 2), rn // 2, c0, cn)
            give = (r0 + (1 - bit) * (rn // 2), rn // 2, c0, cn)
        else:
            keep = (r0, rn, c0 + bit * (cn // 2), cn // 2)
            give = (r0, rn, c0 + (1 - bit) * (cn // 2), cn // 2)
        offset = sum(r if (r // 2) % 8 else r // 2 for r in rn_before[:step])
        slot = recv.at[pl.ds(offset, keep[1]), pl.ds(part * width, keep[3])]
        copy = remote(
            acc.at[rows_ds(give[0], give[1]), local_ds(part, give[2], give[3])],
            slot,
            rs_send.at[part, step],
            rs_recv.at[part, step],
            partners[index],
        )
        copy.start()
        inflight[part, step] = (copy, slot)
        region[part] = keep
        sent[part].append(index)
        pending.append(copy)

    for part in range(parts):
        for i, ref in enumerate(seg_refs):
            pair[part, i].wait_recv()
            spot = (pl.ds(starts[i], rows[i]), pl.ds(part * width, width))
            acc[spot] = ref[:, pl.ds(column(core, part), width)] + pair_recv[spot]
        send_half(part, 0)

    gathers = {}

    def send_whole(part, step):
        r0, rn, c0, cn = region[part]
        spot = out.at[rows_ds(r0, rn), cols_ds(core, part, c0, cn)]
        copy = remote(
            spot, spot, ag_send.at[part, step], ag_recv.at[part, step], partners[sent[part][step]]
        )
        copy.start()
        gathers[part, step] = copy
        pending.append(copy)

    def forward(part, step, r0, rn, c0, cn):
        spot = out.at[rows_ds(r0, rn), cols_ds(core, part, c0, cn)]
        copy = remote(spot, spot, fw_send.at[part, step], fw_recv.at[part, step], other)
        copy.start()
        forwards.append(copy)

    forwards = []
    for step in range(count):
        for part in range(parts):
            copy, slot = inflight[part, step]
            copy.wait_recv()
            r0, rn, c0, cn = region[part]
            spot = (rows_ds(r0, rn), local_ds(part, c0, cn))
            if step < count - 1:
                acc[spot] += slot[...]
                send_half(part, step + 1)
            else:
                out[rows_ds(r0, rn), cols_ds(core, part, c0, cn)] = acc[spot] + slot[...]
                send_whole(part, step)
                forward(part, count, r0, rn, c0, cn)

    for step in reversed(range(count)):
        for part in range(parts):
            gathers[part, step].wait_recv()
            r0, rn, c0, cn = region[part]
            bit = bits[sent[part][step]][0]
            if (rn_before[step]) == rn:
                got = (r0, rn, c0 + (1 - 2 * bit) * cn, cn)
                region[part] = (r0, rn, c0 - bit * cn, 2 * cn)
            else:
                got = (r0 + (1 - 2 * bit) * rn, rn, c0, cn)
                region[part] = (r0 - bit * rn, 2 * rn, c0, cn)
            if step > 0:
                send_whole(part, step - 1)
            forward(part, step, *got)

    for copy in pending:
        copy.wait_send()
    for copy in forwards:
        copy.wait()


def total(sizes, segments):
    rows = tuple(s.shape[0] for s in segments)
    cols = segments[0].shape[1]
    count = sizes[0].bit_length() - 1 + sizes[1].bit_length() - 2
    total_rows = sum(rows)
    parts = 4 if (total_rows >> count) % 8 == 0 else 2
    vmem = pl.BlockSpec(memory_space=pltpu.VMEM)
    dma = lambda *shape: pltpu.SemaphoreType.DMA(shape)
    result = pl.pallas_call(
        functools.partial(total_kernel, sizes, parts, rows, cols),
        out_shape=jax.ShapeDtypeStruct((total_rows, cols), jnp.float32),
        in_specs=[vmem] * len(rows),
        out_specs=vmem,
        scratch_shapes=[
            pltpu.VMEM((total_rows, cols // 2), jnp.float32),
            pltpu.VMEM((total_rows, cols // 2), jnp.float32),
            pltpu.VMEM((total_rows + 64, cols // 2), jnp.float32),
            dma(parts, len(rows)),
            dma(parts, len(rows)),
            dma(parts, count),
            dma(parts, count),
            dma(parts, count),
            dma(parts, count),
            dma(parts, count + 1),
            dma(parts, count + 1),
        ],
        compiler_params=pltpu.CompilerParams(
            collective_id=0, has_side_effects=True, vmem_limit_bytes=48 << 20
        ),
    )(*segments)
    at = 0
    outs = []
    for r in rows:
        outs.append(result[at : at + r])
        at += r
    return outs


def on_device(state_field, diffusion, weight_in, weight_mid, weight_out, block_tile, block_pos):
    levels, tile_rows, tile_cols = state_field.shape
    above, below = halo(state_field, "sim", 1, 2)
    senders = lax.axis_size("sim")
    own_index = lax.axis_index("sim")
    samples = block_tile.shape[0] // senders
    per_row = tile_cols // BW
    tiles = block_tile[:, 0].reshape(senders, samples)
    places = block_pos.reshape(senders, samples)
    matched = tiles == own_index
    place = jnp.sum(jnp.where(matched, places, 0), axis=1)
    present = jnp.any(matched, axis=1)

    def cut(field):
        def piece(spot):
            row = spot // per_row
            start = spot % per_row * BW
            zero = jnp.zeros((), jnp.int32)
            return lax.dynamic_slice(field, (zero, row, start), (levels, 1, BW))[:, 0, :]

        return jax.vmap(piece)(place)

    keep = present[:, None, None]
    cols_in = cut(state_field)
    send_in = jnp.where(keep, jnp.swapaxes(cols_in, 1, 2), 0.0).astype(jnp.bfloat16)
    inputs = send_in.reshape(-1, levels)
    saved = forward(inputs, weight_in, weight_mid)
    above, below, saved = lax.optimization_barrier((above, below, saved))
    output = jnp.dot(
        saved[3], weight_out.astype(jnp.bfloat16), preferred_element_type=jnp.float32
    )
    padded = jnp.concatenate([above, state_field, below], axis=1)
    before, behind = halo(padded, "learn", 2, 2)
    before, behind, output = lax.optimization_barrier((before, behind, output))
    padded = jnp.concatenate([before, padded, behind], axis=2)
    after = interior_step(interior_step(padded, diffusion), diffusion)
    cols_target = cut(after - state_field)
    send_target = jnp.where(keep, TARGET_GAIN * jnp.swapaxes(cols_target, 1, 2), 0.0).astype(
        jnp.bfloat16
    )
    targets = send_target.reshape(-1, levels)
    count = float(senders * lax.axis_size("learn") * samples * BW)
    grad_in, grad_mid, grad_out = gradients(
        inputs, targets, saved, output, weight_mid, weight_out, count
    )
    sizes = (senders, lax.axis_size("learn"))
    total_in, total_mid, total_out = total(sizes, (grad_in, grad_mid, grad_out))
    new_in = weight_in - RATE * total_in
    new_mid = weight_mid - RATE * total_mid
    new_out = weight_out - RATE * total_out.T
    return (after, new_in, new_mid, new_out)


def solution(mesh):
    placed = (P(None, "sim", "learn"), P(), P(), P(), P(), P("learn", None), P("learn"))
    return jax.shard_map(
        on_device,
        mesh=mesh,
        in_specs=placed,
        out_specs=(P(None, "sim", "learn"), P(), P(), P()),
        check_vma=False,
    )
```

```python
import jax
import jax.numpy as jnp
from jax import lax
from jax.experimental import pallas as pl
from jax.experimental.pallas import tpu as pltpu
from jax.sharding import PartitionSpec as P
import functools

BW = 128


RATE = 0.5
TARGET_GAIN = 4.0


def halo(x, axis, dim, width):
    size, length = (lax.axis_size(axis), x.shape[dim])
    up = [(i, (i + 1) % size) for i in range(size)]
    down = [(j, i) for i, j in up]
    last = lax.slice_in_dim(x, length - width, length, axis=dim)
    first = lax.slice_in_dim(x, 0, width, axis=dim)
    before = lax.ppermute(last, axis, up)
    after = lax.ppermute(first, axis, down)
    return before, after


def interior_step(padded, diffusion):
    center = padded[:, 1:-1, 1:-1]
    beside_all = padded[:, :-2, 1:-1] + padded[:, 2:, 1:-1]
    beside_all = beside_all + padded[:, 1:-1, :-2] + padded[:, 1:-1, 2:]
    return center + diffusion[:, None, None] * (beside_all - 4.0 * center)


def silu_slope(value):
    sigma = jax.nn.sigmoid(value)
    return sigma * (1.0 + value * (1.0 - sigma))


def forward(inputs, weight_in, weight_mid):
    first = weight_in.astype(jnp.bfloat16)
    second = weight_mid.astype(jnp.bfloat16)
    pre_one = jnp.dot(inputs, first, preferred_element_type=jnp.float32)
    act_one = jax.nn.silu(pre_one).astype(jnp.bfloat16)
    pre_two = jnp.dot(act_one, second, preferred_element_type=jnp.float32)
    act_two = jax.nn.silu(pre_two).astype(jnp.bfloat16)
    return pre_one, act_one, pre_two, act_two


def gradients(inputs, targets, saved, output, weight_mid, weight_out, count):
    pre_one, act_one, pre_two, act_two = saved
    second = weight_mid.astype(jnp.bfloat16)
    third = weight_out.astype(jnp.bfloat16)
    error = ((output - targets.astype(jnp.float32)) / count).astype(jnp.bfloat16)
    grad_out = jnp.dot(error.T, act_two, preferred_element_type=jnp.float32)
    back_two = jnp.dot(error, third.T, preferred_element_type=jnp.float32)
    delta_two = (back_two * silu_slope(pre_two)).astype(jnp.bfloat16)
    grad_mid = jnp.dot(act_one.T, delta_two, preferred_element_type=jnp.float32)
    back_one = jnp.dot(delta_two, second.T, preferred_element_type=jnp.float32)
    delta_one = (back_one * silu_slope(pre_one)).astype(jnp.bfloat16)
    grad_in = jnp.dot(inputs.T, delta_one, preferred_element_type=jnp.float32)
    return (grad_in, grad_mid, grad_out)


MESH = pl.DeviceIdType.MESH


def total_kernel(sizes, blocks, rows, cols, *refs):
    col_parts, row_parts = blocks
    parts = col_parts * row_parts
    seg_refs = refs[: len(rows)]
    out, acc, pair_recv, recv = refs[len(rows) : len(rows) + 4]
    pair_send_sem, pair_recv_sem, rs_send, rs_recv, ag_send, ag_recv, fw_send, fw_recv = refs[
        len(rows) + 4 :
    ]
    sim_size, learn_size = sizes
    sim, learn = lax.axis_index("sim"), lax.axis_index("learn")
    bits = []
    for step in range(sim_size.bit_length() - 1):
        bits.append((lax.rem(sim // (1 << step), 2), 1 << step, 0))
    for step in range(1, learn_size.bit_length() - 1):
        bits.append((lax.rem(learn // (1 << step), 2), 0, 1 << step))
    count = len(bits)
    near = min(3, count)
    core = lax.rem(learn, 2)
    other = (sim, learn + 1 - 2 * core)
    partners = [(sim + (1 - 2 * b) * ds, learn + (1 - 2 * b) * dl) for b, ds, dl in bits]

    barrier = pltpu.get_barrier_semaphore()
    for partner in partners + [other]:
        pl.semaphore_signal(barrier, inc=1, device_id=partner, device_id_type=MESH)
    pl.semaphore_wait(barrier, count + 1)

    total_rows = sum(rows)
    half = cols // 2
    width = half // col_parts
    tall = total_rows // row_parts
    starts = [sum(rows[:i]) for i in range(len(rows))]

    def column(side, part):
        return pl.multiple_of(side * half + part % col_parts * width, 128)

    def pieces(part):
        low = part // col_parts * tall
        found = []
        for i in range(len(rows)):
            first, last = max(low, starts[i]), min(low + tall, starts[i] + rows[i])
            if first < last:
                found.append((i, first, last - first))
        return found

    def remote(src, dst, send, recv_, device):
        return pltpu.make_async_remote_copy(
            src_ref=src,
            dst_ref=dst,
            send_sem=send,
            recv_sem=recv_,
            device_id=device,
            device_id_type=MESH,
        )

    pending = []
    pair = {}
    for part in range(parts):
        for i, first, number in pieces(part):
            copy = remote(
                seg_refs[i].at[
                    pl.ds(first - starts[i], number), pl.ds(column(1 - core, part), width)
                ],
                pair_recv.at[pl.ds(first, number), pl.ds(part % col_parts * width, width)],
                pair_send_sem.at[part, i],
                pair_recv_sem.at[part, i],
                other,
            )
            copy.start()
            pair[part, i] = copy
            pending.append(copy)

    region = [(part // col_parts * tall, tall, 0, width) for part in range(parts)]
    rn_before, left = [], tall
    for _ in range(count):
        rn_before.append(left)
        left = left // 2 if (left // 2) % 8 == 0 else left
    sent = [[] for _ in range(parts)]

    def rows_ds(r0, rn):
        return pl.ds(r0 if isinstance(r0, int) else pl.multiple_of(r0, 8), rn)

    def cols_ds(side, part, c0, cn):
        return pl.ds(pl.multiple_of(side * half + part % col_parts * width + c0, 128), cn)

    def local_ds(part, c0, cn):
        start = part % col_parts * width + c0
        return pl.ds(start if isinstance(start, int) else pl.multiple_of(start, 128), cn)

    inflight = {}

    def send_half(part, step):
        r0, rn, c0, cn = region[part]
        index = (part + step) % near if step < near else step
        bit = bits[index][0]
        if (rn // 2) % 8 == 0:
            keep = (r0 + bit * (rn // 2), rn // 2, c0, cn)
            give = (r0 + (1 - bit) * (rn // 2), rn // 2, c0, cn)
        else:
            keep = (r0, rn, c0 + bit * (cn // 2), cn // 2)
            give = (r0, rn, c0 + (1 - bit) * (cn // 2), cn // 2)
        offset = sum(r if (r // 2) % 8 else r // 2 for r in rn_before[:step])
        offset += part // col_parts * tall
        slot = recv.at[pl.ds(offset, keep[1]), pl.ds(part % col_parts * width, keep[3])]
        copy = remote(
            acc.at[rows_ds(give[0], give[1]), local_ds(part, give[2], give[3])],
            slot,
            rs_send.at[part, step],
            rs_recv.at[part, step],
            partners[index],
        )
        copy.start()
        inflight[part, step] = (copy, slot)
        region[part] = keep
        sent[part].append(index)
        pending.append(copy)

    for part in range(parts):
        for i, first, number in pieces(part):
            pair[part, i].wait_recv()
            spot = (pl.ds(first, number), pl.ds(part % col_parts * width, width))
            mine = seg_refs[i][
                pl.ds(first - starts[i], number), pl.ds(column(core, part), width)
            ]
            acc[spot] = mine + pair_recv[spot]
        send_half(part, 0)

    gathers = {}

    def send_whole(part, step):
        r0, rn, c0, cn = region[part]
        spot = out.at[rows_ds(r0, rn), cols_ds(core, part, c0, cn)]
        copy = remote(
            spot, spot, ag_send.at[part, step], ag_recv.at[part, step], partners[sent[part][step]]
        )
        copy.start()
        gathers[part, step] = copy
        pending.append(copy)

    def forward(part, step, r0, rn, c0, cn):
        spot = out.at[rows_ds(r0, rn), cols_ds(core, part, c0, cn)]
        copy = remote(spot, spot, fw_send.at[part, step], fw_recv.at[part, step], other)
        copy.start()
        forwards.append(copy)

    forwards = []
    for step in range(count):
        for part in range(parts):
            copy, slot = inflight[part, step]
            copy.wait_recv()
            r0, rn, c0, cn = region[part]
            spot = (rows_ds(r0, rn), local_ds(part, c0, cn))
            if step < count - 1:
                acc[spot] += slot[...]
                send_half(part, step + 1)
            else:
                out[rows_ds(r0, rn), cols_ds(core, part, c0, cn)] = acc[spot] + slot[...]
                send_whole(part, step)
                forward(part, count, r0, rn, c0, cn)

    for step in reversed(range(count)):
        for part in range(parts):
            gathers[part, step].wait_recv()
            r0, rn, c0, cn = region[part]
            bit = bits[sent[part][step]][0]
            if (rn_before[step]) == rn:
                got = (r0, rn, c0 + (1 - 2 * bit) * cn, cn)
                region[part] = (r0, rn, c0 - bit * cn, 2 * cn)
            else:
                got = (r0 + (1 - 2 * bit) * rn, rn, c0, cn)
                region[part] = (r0 - bit * rn, 2 * rn, c0, cn)
            if step > 0:
                send_whole(part, step - 1)
            forward(part, step, *got)

    for copy in pending:
        copy.wait_send()
    for copy in forwards:
        copy.wait()


def total(sizes, segments):
    rows = tuple(s.shape[0] for s in segments)
    cols = segments[0].shape[1]
    count = sizes[0].bit_length() - 1 + sizes[1].bit_length() - 2
    total_rows = sum(rows)
    blocks = (4 if (total_rows >> count) % 8 == 0 else 2, 2 if (total_rows >> count) % 16 == 0 else 1)
    parts = blocks[0] * blocks[1]
    vmem = pl.BlockSpec(memory_space=pltpu.VMEM)
    dma = lambda *shape: pltpu.SemaphoreType.DMA(shape)
    result = pl.pallas_call(
        functools.partial(total_kernel, sizes, blocks, rows, cols),
        out_shape=jax.ShapeDtypeStruct((total_rows, cols), jnp.float32),
        in_specs=[vmem] * len(rows),
        out_specs=vmem,
        scratch_shapes=[
            pltpu.VMEM((total_rows, cols // 2), jnp.float32),
            pltpu.VMEM((total_rows, cols // 2), jnp.float32),
            pltpu.VMEM((total_rows + 64, cols // 2), jnp.float32),
            dma(parts, len(rows)),
            dma(parts, len(rows)),
            dma(parts, count),
            dma(parts, count),
            dma(parts, count),
            dma(parts, count),
            dma(parts, count + 1),
            dma(parts, count + 1),
        ],
        compiler_params=pltpu.CompilerParams(
            collective_id=0, has_side_effects=True, vmem_limit_bytes=48 << 20
        ),
    )(*segments)
    at = 0
    outs = []
    for r in rows:
        outs.append(result[at : at + r])
        at += r
    return outs


def on_device(state_field, diffusion, weight_in, weight_mid, weight_out, block_tile, block_pos):
    levels, tile_rows, tile_cols = state_field.shape
    above, below = halo(state_field, "sim", 1, 2)
    senders = lax.axis_size("sim")
    own_index = lax.axis_index("sim")
    samples = block_tile.shape[0] // senders
    per_row = tile_cols // BW
    tiles = block_tile[:, 0].reshape(senders, samples)
    places = block_pos.reshape(senders, samples)
    matched = tiles == own_index
    place = jnp.sum(jnp.where(matched, places, 0), axis=1)
    present = jnp.any(matched, axis=1)

    def cut(field):
        def piece(spot):
            row = spot // per_row
            start = spot % per_row * BW
            zero = jnp.zeros((), jnp.int32)
            return lax.dynamic_slice(field, (zero, row, start), (levels, 1, BW))[:, 0, :]

        return jax.vmap(piece)(place)

    keep = present[:, None, None]
    cols_in = cut(state_field)
    send_in = jnp.where(keep, jnp.swapaxes(cols_in, 1, 2), 0.0).astype(jnp.bfloat16)
    inputs = send_in.reshape(-1, levels)
    saved = forward(inputs, weight_in, weight_mid)
    above, below, saved = lax.optimization_barrier((above, below, saved))
    output = jnp.dot(
        saved[3], weight_out.astype(jnp.bfloat16), preferred_element_type=jnp.float32
    )
    padded = jnp.concatenate([above, state_field, below], axis=1)
    before, behind = halo(padded, "learn", 2, 2)
    before, behind, output = lax.optimization_barrier((before, behind, output))
    padded = jnp.concatenate([before, padded, behind], axis=2)
    after = interior_step(interior_step(padded, diffusion), diffusion)
    cols_target = cut(after - state_field)
    send_target = jnp.where(keep, TARGET_GAIN * jnp.swapaxes(cols_target, 1, 2), 0.0).astype(
        jnp.bfloat16
    )
    targets = send_target.reshape(-1, levels)
    count = float(senders * lax.axis_size("learn") * samples * BW)
    grad_in, grad_mid, grad_out = gradients(
        inputs, targets, saved, output, weight_mid, weight_out, count
    )
    sizes = (senders, lax.axis_size("learn"))
    total_in, total_mid, total_out = total(sizes, (grad_in, grad_mid, grad_out))
    new_in = weight_in - RATE * total_in
    new_mid = weight_mid - RATE * total_mid
    new_out = weight_out - RATE * total_out.T
    return (after, new_in, new_mid, new_out)


def solution(mesh):
    placed = (P(None, "sim", "learn"), P(), P(), P(), P(), P("learn", None), P("learn"))
    return jax.shard_map(
        on_device,
        mesh=mesh,
        in_specs=placed,
        out_specs=(P(None, "sim", "learn"), P(), P(), P()),
        check_vma=False,
    )
```
